512 devices in a mesh: ka: 16 (over y_lo, z), grid: 32 (over x, y_hi, core).
Axes of the slice: x: 4, y: 8 (y_hi: 4, y_lo: 2; y = y_hi * 2 + y_lo), z: 8, core: 2. Of those that a mesh axis runs over, the one named last changes fastest.
Arguments:
- orbitals: bfloat16 [16, 2, 32768, 256], P('ka', None, 'grid'), may hold values from -0.4453125 to 0.4453125
- fields: bfloat16 [2, 3, 2, 32768], P(None, None, None, 'grid'), may hold values from -6 to 6
- partner: int32 [2, 16], replicated, may hold values from 0 to 15, each once within a row
Outputs:
- coupling: float32 [256, 2, 3, 2, 16, 256], P('grid', None, None, None, 'ka')
The draws below stay inside these ranges and needn't reach their ends.
Inputs may be any that keep to these rules, and one draw needn't show every extreme that they name: Each row of partner names every k-point once.
All inputs are finite; a program needn't handle non-finite values.
Results may differ from the reference program's by a relative error of at most 0.0029.
Values may be sent and summed in bfloat16 or wider, within the bound.
No kernel may reach another device: no remote copies, remote signals or barrier semaphores. Data moves between devices by JAX's collectives and lax.ppermute only.
A program may use at most 64 MiB of HBM per device.

```python
import jax
import jax.numpy as jnp
from jax import lax

B = 256
NU = 3
Q = 2
K = 16
GRID = 32768


def levels(own_key, dims, split, least, largest):
    def one(position, shards_of):
        steps = jax.random.uniform(jax.random.fold_in(jax.random.fold_in(own_key, 6), position), (shards_of,), jnp.float32, least / len(split), largest / len(split))
        return jnp.repeat(jnp.exp(steps), dims[position] // shards_of).reshape((-1,) + (1,) * (len(dims) - position - 1))

    gain = one(*split[0])
    for cut in split[1:]:
        gain = gain * one(*cut)
    return gain


def gaussian(own_key, shape, deviation, most, cuts=(), kind=jnp.bfloat16):
    entries = jax.random.normal(own_key, shape, jnp.float32) * deviation
    if len(cuts) > 0:
        entries = levels(own_key, shape, cuts, -0.22, 0.18) * entries
    return jnp.clip(entries, min=-most, max=most).astype(kind)


def setup_inputs(seed: int = 0) -> dict:
    streams_of = jax.random.split(jax.random.key(seed), 4)
    return {
        "orbitals": gaussian(streams_of[0], (K, 2, GRID, B), (GRID ** -0.25), 0.4453125, ((0, 16), (2, 32))),
        "fields": gaussian(streams_of[1], (Q, NU, 2, GRID), 1.0, 6.0, ((3, 32),)),
        "partner": jax.vmap(lambda own: jax.random.permutation(own, K))(jax.random.split(streams_of[2], Q)).reshape((Q, K)).astype(jnp.int32),
    }


def weigh_orbitals(field_pair, own):
    field_real = field_pair[:, 0, :].astype(jnp.float32).T
    field_imag = field_pair[:, 1, :].astype(jnp.float32).T
    own_real = own[0].astype(jnp.float32)[:, None, :]
    own_imag = own[1].astype(jnp.float32)[:, None, :]
    part_real = field_real[:, :, None] * own_real - field_imag[:, :, None] * own_imag
    part_imag = field_real[:, :, None] * own_imag + field_imag[:, :, None] * own_real
    weighted = jnp.stack([part_real, part_imag], axis=1).astype(jnp.bfloat16)
    return weighted.reshape(weighted.shape[0], -1)


def couple_block(fetched_rows, weighted, modes, bands):
    row_count = fetched_rows.shape[2]
    stacked = jnp.concatenate([fetched_rows[0], fetched_rows[1]], axis=1)
    product = jnp.dot(stacked.T, weighted, preferred_element_type=jnp.float32)
    product = product.reshape(2, row_count, 2, modes, bands)
    part_real = product[0, :, 0] + product[1, :, 1]
    part_imag = product[0, :, 1] - product[1, :, 0]
    return jnp.stack([part_real, part_imag], axis=2)


def reference(orbitals, fields, partner):
    results = []
    for which in range(Q):
        def per_point(kpoint):
            fetched = lax.dynamic_index_in_dim(orbitals, partner[which, kpoint], 0, keepdims=False)
            own = lax.dynamic_index_in_dim(orbitals, kpoint, 0, keepdims=False)
            weighted = weigh_orbitals(fields[which], own)
            return couple_block(fetched, weighted, NU, B)

        blocks = lax.map(per_point, jnp.arange(K, dtype=jnp.int32))
        results.append(jnp.transpose(blocks, (1, 2, 3, 0, 4)))
    return jnp.stack(results, axis=1)
```

```python
import jax
import jax.numpy as jnp
from jax import lax
from jax.sharding import Mesh, PartitionSpec as P

KA = ("ylo", "z")
GRID = ("x", "yhi", "core")


def weigh(field_pair, own):
    modes = field_pair.shape[0]
    rows = own.shape[1]
    field_real = field_pair[:, 0, :].astype(jnp.float32).T[:, :, None]
    field_imag = field_pair[:, 1, :].astype(jnp.float32).T[:, :, None]
    own_real = own[0].astype(jnp.float32)[:, None, :]
    own_imag = own[1].astype(jnp.float32)[:, None, :]
    part_real = (field_real * own_real - field_imag * own_imag).astype(jnp.bfloat16)
    part_imag = (field_real * own_imag + field_imag * own_real).astype(jnp.bfloat16)
    upper = jnp.stack([part_real, part_imag], axis=2)
    lower = jnp.stack([part_imag, -part_real], axis=2)
    return jnp.stack([upper, lower], axis=0).reshape(2 * rows, -1)


def reduce_scatter(product):
    bands, width = product.shape
    core = lax.axis_size("core")
    xs = lax.axis_size("x")
    ys = lax.axis_size("yhi")
    keep = bands // (core * xs * ys)
    parts = product.reshape(xs, ys, core, keep, width)
    parts = lax.all_to_all(parts, "core", split_axis=2, concat_axis=2, tiled=True)
    parts = parts.sum(axis=2).astype(jnp.bfloat16)
    parts = lax.all_to_all(parts, "x", split_axis=0, concat_axis=0, tiled=True)
    parts = parts.astype(jnp.float32).sum(axis=0)
    parts = lax.all_to_all(parts, "yhi", split_axis=0, concat_axis=0, tiled=True)
    return parts.sum(axis=0)


def per_device(orbitals, fields, partner):
    num_q, modes = fields.shape[:2]
    own = orbitals[0]
    rows, bands = own.shape[1:]
    points = lax.axis_size(KA)
    flat = own.reshape(points, 2 * rows // points, bands)
    spread = lax.all_to_all(flat, KA, split_axis=0, concat_axis=0, tiled=True)
    results = []
    fetched = None
    for which in range(num_q):
        picked = spread.at[partner[which]].get(mode="promise_in_bounds")
        if fetched is not None:
            picked, fetched = lax.optimization_barrier((picked, fetched))
            results.append(finish(fetched, weighted))
        fetched = lax.all_to_all(picked, KA, split_axis=0, concat_axis=0, tiled=True)
        weighted = weigh(fields[which], own)
    results.append(finish(fetched, weighted))
    keep = results[0].shape[0]
    parts = [r.reshape(keep, modes, 2, 1, bands) for r in results]
    return jnp.stack(parts, axis=1)


def finish(fetched, weighted):
    lhs = fetched.reshape(-1, fetched.shape[-1])
    product = lax.dot_general(lhs, weighted, (((0,), (0,)), ((), ())), preferred_element_type=jnp.float32)
    return reduce_scatter(product)


def solution(mesh):
    fine = Mesh(mesh.devices.reshape(2, 8, 4, 4, 2), KA + GRID)
    return jax.shard_map(
        per_device,
        mesh=fine,
        in_specs=(P(KA, None, GRID, None), P(None, None, None, GRID), P()),
        out_specs=P(GRID, None, None, None, KA, None),
        check_vma=False,
    )
```

```python
import functools

import jax
import jax.numpy as jnp
from jax import lax
from jax.experimental import pallas as pl
from jax.experimental.pallas import tpu as pltpu
from jax.sharding import Mesh, PartitionSpec as P


KA = ("ylo", "z")
GRID = ("x", "yhi", "core")


def near(value):
    return pltpu.with_memory_space_constraint(value, pltpu.VMEM)


def weigh_kernel(fields_ref, own_ref, out_ref):
    num_q, _, _, width = out_ref.shape
    bands = own_ref.shape[-1]
    modes = width // (2 * bands)
    own_real = own_ref[0].astype(jnp.float32)
    own_imag = own_ref[1].astype(jnp.float32)
    for which in range(num_q):
        for mode in range(modes):
            at = 2 * (which * modes + mode)
            field_real = fields_ref[:, at : at + 1]
            field_imag = fields_ref[:, at + 1 : at + 2]
            part_real = (field_real * own_real - field_imag * own_imag).astype(jnp.bfloat16)
            part_imag = (field_real * own_imag + field_imag * own_real).astype(jnp.bfloat16)
            first = pl.ds(2 * mode * bands, bands)
            second = pl.ds((2 * mode + 1) * bands, bands)
            out_ref[which, 0, :, first] = part_real
            out_ref[which, 0, :, second] = part_imag
            out_ref[which, 1, :, first] = part_imag
            out_ref[which, 1, :, second] = -part_real


def weigh(fields, own, block=128):
    num_q, modes, _, rows = fields.shape
    bands = own.shape[-1]
    width = 2 * modes * bands
    columns = fields.reshape(num_q * modes * 2, rows).astype(jnp.float32).T
    out = pl.pallas_call(
        weigh_kernel,
        grid=(rows // block,),
        in_specs=[
            pl.BlockSpec((block, num_q * modes * 2), lambda i: (i, 0)),
            pl.BlockSpec((2, block, bands), lambda i: (0, i, 0)),
        ],
        out_specs=pl.BlockSpec((num_q, 2, block, width), lambda i: (0, 0, i, 0)),
        out_shape=jax.ShapeDtypeStruct((num_q, 2, rows, width), jnp.bfloat16),
        name="weigh",
    )(columns, own)
    return out.reshape(num_q, 2 * rows, width)


def couple_kernel(core_ref, fetched_ref, weighted_ref, keep_ref, send_ref, turned_ref, block_ref):
    @pl.when(pl.program_id(0) == 0)
    def _():
        turned_ref[...] = fetched_ref[...].T

    block_ref[...] = jnp.dot(turned_ref[...], weighted_ref[0], preferred_element_type=jnp.float32)
    pieces, rows, _ = keep_ref.shape
    cols = pl.ds(pl.multiple_of(pl.program_id(0) * block_ref.shape[1], 128), block_ref.shape[1])
    mine = core_ref[0] * rows
    other = rows - mine
    for piece in range(pieces):
        start = 2 * rows * piece
        keep_ref[piece, :, cols] = block_ref[pl.ds(pl.multiple_of(start + mine, 8), rows), :]
        send_ref[piece, :, cols] = block_ref[pl.ds(pl.multiple_of(start + other, 8), rows), :]


def couple(which, fetched, weighted, block=256):
    depth, bands = fetched.shape
    width = weighted.shape[-1]
    pieces = lax.axis_size("x") * lax.axis_size("yhi")
    rows = bands // (2 * pieces)
    half = pltpu.VMEM((pieces, rows, width), jnp.float32)
    return pl.pallas_call(
        couple_kernel,
        grid_spec=pltpu.PrefetchScalarGridSpec(
            num_scalar_prefetch=1,
            grid=(width // block,),
            in_specs=[
                pl.BlockSpec(memory_space=pltpu.VMEM),
                pl.BlockSpec((1, depth, block), lambda j, core: (which, 0, j)),
            ],
            out_specs=[pl.BlockSpec(memory_space=pltpu.VMEM)] * 2,
            scratch_shapes=[pltpu.VMEM((bands, depth), jnp.bfloat16), pltpu.VMEM((bands, block), jnp.float32)],
        ),
        out_shape=[half, half],
        name="couple",
    )(lax.axis_index("core").astype(jnp.int32).reshape(1), near(fetched), weighted)


def fold_kernel(x_ref, keep_ref, received_ref, *out_refs):
    count = len(out_refs)
    span = out_refs[0].shape[0]
    for shift, out_ref in enumerate(out_refs):
        start = lax.rem(x_ref[0] + shift, count) * span
        for piece in range(span):
            out_ref[piece] = (keep_ref[start + piece] + received_ref[start + piece]).astype(out_ref.dtype)


def fold(keep, received):
    xs = lax.axis_size("x")
    pieces, rows, width = keep.shape
    out = pltpu.VMEM((pieces // xs, rows, width), jnp.bfloat16)
    return pl.pallas_call(
        fold_kernel,
        grid_spec=pltpu.PrefetchScalarGridSpec(
            num_scalar_prefetch=1,
            grid=(),
            in_specs=[pl.BlockSpec(memory_space=pltpu.VMEM)] * 2,
            out_specs=[pl.BlockSpec(memory_space=pltpu.VMEM)] * xs,
        ),
        out_shape=[out] * xs,
        name="fold",
    )(lax.axis_index("x").astype(jnp.int32).reshape(1), near(keep), near(received))


def gather_x_kernel(counts, *refs):
    out_ref = refs[-1]
    start = 0
    for which, count in enumerate(counts):
        mine = refs[start : start + count]
        start += count
        for piece in range(out_ref.shape[0]):
            total = mine[0][piece].astype(jnp.float32)
            for ref in mine[1:]:
                total = total + ref[piece].astype(jnp.float32)
            out_ref[piece, which] = total


def gather_x(groups):
    span, rows, width = groups[0][0].shape
    flat = [part for group in groups for part in group]
    return pl.pallas_call(
        functools.partial(gather_x_kernel, tuple(len(group) for group in groups)),
        in_specs=[pl.BlockSpec(memory_space=pltpu.VMEM)] * len(flat),
        out_specs=pl.BlockSpec(memory_space=pltpu.VMEM),
        out_shape=pltpu.VMEM((span, len(groups), rows, width), jnp.float32),
        name="gather_x",
    )(*[near(part) for part in flat])


def final_kernel(parts_ref, out_ref):
    count, num_q, rows, _ = parts_ref.shape
    _, _, modes, _, _, bands = out_ref.shape
    for which in range(num_q):
        for col in range(2 * modes):
            cols = pl.ds(col * bands, bands)
            total = parts_ref[0, which, :, cols]
            for source in range(1, count):
                total = total + parts_ref[source, which, :, cols]
            for row in range(rows):
                out_ref[row, which, col // 2, col % 2] = total[row : row + 1]


def final(parts, modes):
    _, num_q, rows, width = parts.shape
    bands = width // (2 * modes)
    return pl.pallas_call(
        final_kernel,
        in_specs=[pl.BlockSpec(memory_space=pltpu.VMEM)],
        out_specs=pl.BlockSpec(memory_space=pltpu.VMEM),
        out_shape=jax.ShapeDtypeStruct((rows, num_q, modes, 2, 1, bands), jnp.float32),
        name="final",
    )(near(parts))


def pick_kernel(partner_ref, spread_ref, out_ref, sems):
    count = out_ref.shape[0]
    copies = [
        pltpu.make_async_copy(spread_ref.at[partner_ref[at]], out_ref.at[at], sems.at[at]) for at in range(count)
    ]
    for copy in copies:
        copy.start()
    for copy in copies:
        copy.wait()


def pick(spread, partner):
    return pl.pallas_call(
        pick_kernel,
        grid_spec=pltpu.PrefetchScalarGridSpec(
            num_scalar_prefetch=1,
            grid=(),
            in_specs=[pl.BlockSpec(memory_space=pltpu.VMEM)],
            out_specs=pl.BlockSpec(memory_space=pl.ANY),
            scratch_shapes=[pltpu.SemaphoreType.DMA((spread.shape[0],))],
        ),
        out_shape=jax.ShapeDtypeStruct(spread.shape, spread.dtype),
        name="pick",
    )(partner, near(spread))


def reduce_core_x(which, fetched, weighted):
    keep, send = couple(which, fetched, weighted)
    received = lax.ppermute(send, "core", [(0, 1), (1, 0)])
    parts = fold(keep, received)
    count = len(parts)
    moved = [
        lax.ppermute(parts[shift], "x", [(at, (at + shift) % count) for at in range(count)])
        for shift in range(1, count)
    ]
    return [parts[0], *moved]


def exchange(value, axis):
    return lax.all_to_all(value, axis, split_axis=0, concat_axis=0, tiled=True)


def per_device(orbitals, fields, partner):
    num_q, modes = fields.shape[:2]
    own = orbitals[0]
    rows, bands = own.shape[1:]
    points = lax.axis_size(KA)
    flat = own.reshape(points, 2 * rows // points, bands)
    spread = exchange(flat, KA)
    weighted = weigh(fields, own)
    picked = []
    for which in range(num_q):
        picked.append(pick(spread, partner[which]))
    fetched = []
    for which in range(num_q):
        if which:
            picked[which], fetched[-1] = lax.optimization_barrier((picked[which], fetched[-1]))
        fetched.append(exchange(picked[which], KA))
    groups = [reduce_core_x(which, fetched[which].reshape(2 * rows, bands), weighted) for which in range(num_q)]
    for which in range(num_q - 1):
        groups[which] = [gather_x([groups[which]])[:, 0]]
    parts = gather_x(groups)
    parts = exchange(parts, "yhi")
    return final(parts, modes)


def solution(mesh):
    fine = Mesh(mesh.devices.reshape(2, 8, 4, 4, 2), KA + GRID)

    return jax.shard_map(
        per_device,
        mesh=fine,
        in_specs=(P(KA, None, GRID, None), P(None, None, None, GRID), P()),
        out_specs=P(GRID, None, None, None, KA, None),
        check_vma=False,
    )
```

```python
import jax
import jax.numpy as jnp
from jax import lax
from jax.experimental import pallas as pl
from jax.experimental.pallas import tpu as pltpu
from jax.sharding import Mesh, PartitionSpec as P


KA = ("ylo", "z")
GRID = ("x", "yhi", "core")
WHOLE = pl.BlockSpec(memory_space=pltpu.VMEM)
PARAMS = pltpu.CompilerParams(vmem_limit_bytes=16 << 20)


def far(value):
    return pltpu.with_memory_space_constraint(value, pltpu.HBM)


def near(value):
    return pltpu.with_memory_space_constraint(value, pltpu.VMEM)


def weigh_kernel(fields_ref, own_ref, out_ref):
    bands = own_ref.shape[-1]
    own_real = own_ref[0].astype(jnp.float32)
    own_imag = own_ref[1].astype(jnp.float32)
    for mode in range(out_ref.shape[-1] // bands):
        field_real = fields_ref[:, 2 * mode : 2 * mode + 1]
        field_imag = fields_ref[:, 2 * mode + 1 : 2 * mode + 2]
        cols = slice(mode * bands, (mode + 1) * bands)
        out_ref[0, :, cols] = (field_real * own_real - field_imag * own_imag).astype(jnp.bfloat16)
        out_ref[1, :, cols] = (field_real * own_imag + field_imag * own_real).astype(jnp.bfloat16)


def weigh(field, own, block=256):
    modes, _, rows = field.shape
    bands = own.shape[-1]
    columns = field.reshape(modes * 2, rows).astype(jnp.float32).T
    out = pl.pallas_call(
        weigh_kernel,
        grid=(rows // block,),
        in_specs=[
            pl.BlockSpec((block, modes * 2), lambda i: (i, 0)),
            pl.BlockSpec((2, block, bands), lambda i: (0, i, 0)),
        ],
        out_specs=pl.BlockSpec((2, block, modes * bands), lambda i: (0, i, 0)),
        out_shape=pltpu.HBM((2, rows, modes * bands), jnp.bfloat16),
        compiler_params=PARAMS,
        name="weigh",
    )(columns, own)
    return out.reshape(2 * rows, modes * bands)


def pick_kernel(partner_ref, spread_ref, out_ref):
    for which in range(out_ref.shape[0]):
        for at in range(out_ref.shape[1]):
            out_ref[which, at] = spread_ref[partner_ref[which, at]]


def pick(spread, partner):
    return pl.pallas_call(
        pick_kernel,
        grid_spec=pltpu.PrefetchScalarGridSpec(num_scalar_prefetch=1, grid=(), in_specs=[WHOLE], out_specs=WHOLE),
        out_shape=pltpu.VMEM(partner.shape + spread.shape[1:], spread.dtype),
        compiler_params=PARAMS,
        name="pick",
    )(partner, near(spread))


def turn(fetched_ref, left_ref):
    bands = fetched_ref.shape[1]
    rows = fetched_ref.shape[0] // 2
    turned = fetched_ref[...].T
    left_ref[:bands] = turned
    left_ref[bands:, :rows] = -turned[:, rows:]
    left_ref[bands:, rows:] = turned[:, :rows]


def couple_kernel(core_ref, fetched_ref, own_ref, other_hbm, out_ref, left_ref, sum_ref, other_ref, sem):
    copy = pltpu.make_async_copy(other_hbm, other_ref, sem)
    copy.start()
    pieces, rows, width = out_ref.shape
    bands = pieces * rows
    turn(fetched_ref.at[core_ref[0]], left_ref.at[0])
    turn(fetched_ref.at[1 - core_ref[0]], left_ref.at[1])
    for start in range(0, width // 2, bands):
        cols = slice(start, start + bands)
        sum_ref[:, cols] = jnp.dot(left_ref[0], own_ref[:, cols], preferred_element_type=jnp.float32)
    copy.wait()
    for start in range(0, width // 2, bands):
        cols = slice(start, start + bands)
        total = sum_ref[:, cols] + jnp.dot(left_ref[1], other_ref[:, cols], preferred_element_type=jnp.float32)
        total = total.astype(out_ref.dtype).reshape(2, pieces, rows, bands)
        for part in range(2):
            at = 2 * start + part * bands
            out_ref[:, :, at : at + bands] = total[part]


def couple(core, fetched, own, other):
    _, depth, bands = fetched.shape
    width = own.shape[-1]
    pieces = lax.axis_size(GRID)
    return pl.pallas_call(
        couple_kernel,
        grid_spec=pltpu.PrefetchScalarGridSpec(
            num_scalar_prefetch=1,
            grid=(),
            in_specs=[WHOLE, WHOLE, pl.BlockSpec(memory_space=pltpu.HBM)],
            out_specs=WHOLE,
            scratch_shapes=[
                pltpu.VMEM((2, 2 * bands, depth), jnp.bfloat16),
                pltpu.VMEM((2 * bands, width), jnp.float32),
                pltpu.VMEM(other.shape, other.dtype),
                pltpu.SemaphoreType.DMA(()),
            ],
        ),
        out_shape=pltpu.VMEM((pieces, bands // pieces, 2 * width), jnp.bfloat16),
        compiler_params=PARAMS,
        name="couple",
    )(core.astype(jnp.int32).reshape(1), near(fetched), near(own), far(other))


def final_kernel(parts_ref, out_ref):
    rows, num_q, modes, _, _, bands = out_ref.shape
    for which in range(num_q):
        for col in range(2 * modes):
            cols = slice(col * bands, (col + 1) * bands)
            total = parts_ref[which, :, cols].astype(jnp.float32)
            for source in range(which + num_q, parts_ref.shape[0], num_q):
                total = total + parts_ref[source, :, cols].astype(jnp.float32)
            for row in range(rows):
                out_ref[row, which, col // 2, col % 2] = total[row : row + 1]


def final(parts, num_q, modes):
    _, rows, width = parts.shape
    return pl.pallas_call(
        final_kernel,
        in_specs=[WHOLE],
        out_specs=WHOLE,
        out_shape=jax.ShapeDtypeStruct((rows, num_q, modes, 2, 1, width // (2 * modes)), jnp.float32),
        compiler_params=PARAMS,
        name="final",
    )(near(parts))


def exchange(value, axis):
    return lax.all_to_all(value, axis, split_axis=0, concat_axis=0, tiled=True)


def swap(value):
    return lax.ppermute(value, "core", [(0, 1), (1, 0)])


def per_device(orbitals, fields, partner):
    num_q, modes = fields.shape[:2]
    own = orbitals[0]
    rows, bands = own.shape[1:]
    points = lax.axis_size(KA)
    depth = 2 * rows // points
    core = lax.axis_index("core")
    spread = exchange(own.reshape(points, depth, bands), KA)
    other = swap(own)
    other_field = swap(lax.dynamic_index_in_dim(fields, 1 - core, 0, keepdims=False))
    field = lax.dynamic_index_in_dim(fields, core, 0, keepdims=False)
    own_weighted = weigh(field, own)
    other_weighted = weigh(other_field, other)
    picked = pick(spread, partner)
    fetched = exchange(picked.reshape(num_q * points, depth, bands), ("core",) + KA)
    product = couple(core, fetched.reshape(2, 2 * rows, bands), own_weighted, other_weighted)
    parts = exchange(product, GRID)
    return final(parts, num_q, modes)


def solution(mesh):
    fine = Mesh(mesh.devices.reshape(2, 8, 4, 4, 2), KA + GRID)

    return jax.shard_map(
        per_device,
        mesh=fine,
        in_specs=(P(KA, None, GRID, None), P(None, None, None, GRID), P()),
        out_specs=P(GRID, None, None, None, KA, None),
        check_vma=False,
    )
```

```python
import jax
import jax.numpy as jnp
from jax import lax
from jax.experimental import pallas as pl
from jax.experimental.pallas import tpu as pltpu
from jax.sharding import Mesh, PartitionSpec as P


KA = ("ylo", "z")
GRID = ("xhi", "xlo", "yhi", "core")
TEAM = ("xlo", "core")
REDUCE = ("xhi", "yhi", "core")
WHOLE = pl.BlockSpec(memory_space=pltpu.VMEM)
PARAMS = pltpu.CompilerParams(vmem_limit_bytes=24 << 20)


def far(value):
    return pltpu.with_memory_space_constraint(value, pltpu.HBM)


def near(value):
    return pltpu.with_memory_space_constraint(value, pltpu.VMEM)


def weigh_kernel(fields_ref, own_ref, out_ref):
    bands = own_ref.shape[-1]
    own_real = own_ref[0].astype(jnp.float32)
    own_imag = own_ref[1].astype(jnp.float32)
    for mode in range(out_ref.shape[-1] // bands):
        field_real = fields_ref[:, 2 * mode : 2 * mode + 1]
        field_imag = fields_ref[:, 2 * mode + 1 : 2 * mode + 2]
        cols = slice(mode * bands, (mode + 1) * bands)
        out_ref[0, :, cols] = (field_real * own_real - field_imag * own_imag).astype(jnp.bfloat16)
        out_ref[1, :, cols] = (field_real * own_imag + field_imag * own_real).astype(jnp.bfloat16)


def weigh(field, own, block=256):
    modes, _, rows = field.shape
    bands = own.shape[-1]
    columns = field.reshape(modes * 2, rows).astype(jnp.float32).T
    out = pl.pallas_call(
        weigh_kernel,
        grid=(rows // block,),
        in_specs=[
            pl.BlockSpec((block, modes * 2), lambda i: (i, 0)),
            pl.BlockSpec((2, block, bands), lambda i: (0, i, 0)),
        ],
        out_specs=pl.BlockSpec((2, block, modes * bands), lambda i: (0, i, 0)),
        out_shape=pltpu.HBM((2, rows, modes * bands), jnp.bfloat16),
        compiler_params=PARAMS,
        name="weigh",
    )(columns, own)
    return out.reshape(2 * rows, modes * bands)


def pick_kernel(partner_ref, spread_ref, out_hbm, out_ref, sems):
    num_q, points = out_ref.shape[1:3]
    lanes = out_ref.shape[-1]
    quarter = lanes // 2
    step = points // 4
    low = lax.broadcasted_iota(jnp.int32, out_ref.shape[3:], 1) < quarter
    copies = []
    for which in range(num_q):
        for at in range(points):
            block = spread_ref[partner_ref[which, at]].astype(jnp.float32)
            left, right = block[:, :lanes], block[:, lanes:]
            even = jnp.where(low, left, pltpu.roll(right, quarter, 1))
            odd = jnp.where(low, pltpu.roll(left, quarter, 1), right)
            out_ref[0, which, at] = even.astype(out_ref.dtype)
            out_ref[1, which, at] = odd.astype(out_ref.dtype)
            if (at + 1) % step == 0:
                span = pl.ds(at + 1 - step, step)
                for half in range(2):
                    copies.append(
                        pltpu.make_async_copy(
                            out_ref.at[half, which, span],
                            out_hbm.at[half, which, span],
                            sems.at[half, which, at // step],
                        )
                    )
                    copies[-1].start()
    for copy in copies:
        copy.wait()


def pick(spread, partner):
    _, depth, bands = spread.shape
    shape = (2,) + partner.shape + (depth, bands // 2)
    return pl.pallas_call(
        pick_kernel,
        grid_spec=pltpu.PrefetchScalarGridSpec(
            num_scalar_prefetch=1,
            grid=(),
            in_specs=[WHOLE],
            out_specs=pl.BlockSpec(memory_space=pltpu.HBM),
            scratch_shapes=[pltpu.VMEM(shape, spread.dtype), pltpu.SemaphoreType.DMA((2, partner.shape[0], 4))],
        ),
        out_shape=pltpu.HBM(shape, spread.dtype),
        compiler_params=PARAMS,
        name="pick",
    )(partner, near(spread))


def turn(fetched_ref, left_ref):
    rows = fetched_ref.shape[0] // 2
    bands = fetched_ref.shape[1]
    turned = fetched_ref[...].T
    left_ref[:bands] = turned
    left_ref[bands:, :rows] = -turned[:, rows:]
    left_ref[bands:, rows:] = turned[:, :rows]


def couple_kernel(place_ref, fetched_hbm, own_ref, *refs):
    sides = fetched_hbm.shape[0]
    others_hbm, refs = refs[: sides - 1], refs[sides - 1 :]
    out_ref, fetched_ref, left_ref, sum_ref, others_ref, sems = refs
    pieces, rows, width = out_ref.shape
    block = width // 6
    incoming = [
        pltpu.make_async_copy(
            fetched_hbm.at[lax.bitwise_xor(place_ref[0], side)], fetched_ref.at[side], sems.at[0, side]
        )
        for side in range(sides)
    ]
    weights = [None] + [
        pltpu.make_async_copy(others_hbm[side - 1], others_ref.at[side - 1], sems.at[1, side])
        for side in range(1, sides)
    ]
    for copy in incoming[:2] + weights[1:2] + incoming[2:] + weights[2:3]:
        copy.start()
    for side in range(sides):
        incoming[side].wait()
        turn(fetched_ref.at[side], left_ref.at[side])
        if side:
            weights[side].wait()
            if side + 2 < sides:
                weights[side + 2].start()
        weighted_ref = others_ref.at[side - 1] if side else own_ref
        for start in range(0, width // 2, block):
            cols = slice(start, start + block)
            total = jnp.dot(left_ref[side], weighted_ref[:, cols], preferred_element_type=jnp.float32)
            if side:
                total += sum_ref[:, cols]
            if side < sides - 1:
                sum_ref[:, cols] = total
                continue
            total = total.astype(out_ref.dtype).reshape(2, pieces, rows, block)
            for part in range(2):
                at = 2 * start + part * block
                out_ref[:, :, at : at + block] = total[part]


def couple(place, fetched, own, others):
    sides, depth, bands = fetched.shape
    width = own.shape[-1]
    pieces = lax.axis_size(REDUCE)
    far_spec = pl.BlockSpec(memory_space=pltpu.HBM)
    return pl.pallas_call(
        couple_kernel,
        grid_spec=pltpu.PrefetchScalarGridSpec(
            num_scalar_prefetch=1,
            grid=(),
            in_specs=[far_spec, WHOLE] + [far_spec] * len(others),
            out_specs=WHOLE,
            scratch_shapes=[
                pltpu.VMEM(fetched.shape, fetched.dtype),
                pltpu.VMEM((sides, 2 * bands, depth), jnp.bfloat16),
                pltpu.VMEM((2 * bands, width), jnp.float32),
                pltpu.VMEM((len(others),) + own.shape, own.dtype),
                pltpu.SemaphoreType.DMA((2, sides)),
            ],
        ),
        out_shape=pltpu.VMEM((pieces, bands // pieces, 2 * width), jnp.bfloat16),
        compiler_params=PARAMS,
        name="couple",
    )(place.astype(jnp.int32).reshape(1), far(fetched), near(own), *[far(other) for other in others])


def final_kernel(parts_ref, out_ref):
    rows, num_q, modes, _, _, bands = out_ref.shape
    for which in range(num_q):
        for col in range(2 * modes):
            cols = slice(col * bands, (col + 1) * bands)
            total = parts_ref[which, :, cols].astype(jnp.float32)
            for source in range(which + num_q, parts_ref.shape[0], num_q):
                total = total + parts_ref[source, :, cols].astype(jnp.float32)
            for row in range(rows):
                out_ref[row, which, col // 2, col % 2] = total[row : row + 1]


def final(parts, num_q, modes):
    _, rows, width = parts.shape
    return pl.pallas_call(
        final_kernel,
        in_specs=[WHOLE],
        out_specs=WHOLE,
        out_shape=jax.ShapeDtypeStruct((rows, num_q, modes, 2, 1, width // (2 * modes)), jnp.float32),
        compiler_params=PARAMS,
        name="final",
    )(near(parts))


def exchange(value, axis):
    return lax.all_to_all(value, axis, split_axis=0, concat_axis=0, tiled=True)


def swap(value, axis):
    return lax.ppermute(value, axis, [(0, 1), (1, 0)])


def per_device(orbitals, fields, partner):
    num_q, modes = fields.shape[:2]
    own = orbitals[0]
    rows, bands = own.shape[1:]
    points = lax.axis_size(KA)
    depth = 2 * rows // points
    core = lax.axis_index("core")

    def of_q(values, which):
        return lax.dynamic_index_in_dim(values, which, 0, keepdims=False)

    spread = exchange(own.reshape(points, depth, bands), KA)
    across = swap(own, "xlo")
    across_fields = swap(fields, "xlo")
    beside = swap(own, "core")
    beside_field = swap(of_q(fields, 1 - core), "core")
    corner = swap(across, "core")
    corner_field = swap(of_q(across_fields, 1 - core), "core")
    own_weighted = weigh(of_q(fields, core), own)
    beside_weighted = weigh(beside_field, beside)
    across_weighted = weigh(of_q(across_fields, core), across)
    corner_weighted = weigh(corner_field, corner)
    picked = pick(spread, partner)
    fetched = exchange(picked.reshape(2 * num_q * points, depth, bands // 2), TEAM + KA)
    product = couple(
        lax.axis_index(TEAM),
        fetched.reshape(2 * num_q, 2 * rows, bands // 2),
        own_weighted,
        [beside_weighted, across_weighted, corner_weighted],
    )
    parts = exchange(product, REDUCE)
    return final(parts, num_q, modes)


def solution(mesh):
    fine = Mesh(mesh.devices.reshape(2, 8, 2, 2, 4, 2), KA + GRID)

    return jax.shard_map(
        per_device,
        mesh=fine,
        in_specs=(P(KA, None, GRID, None), P(None, None, None, GRID), P()),
        out_specs=P(GRID, None, None, None, KA, None),
        check_vma=False,
    )
```

```python
import jax
import jax.numpy as jnp
from jax import lax
from jax.experimental import pallas as pl
from jax.experimental.pallas import tpu as pltpu
from jax.sharding import Mesh, PartitionSpec as P


KA = ("ylo", "z")
GRID = ("xhi", "xlo", "yhi", "core")
TEAM = ("xlo", "core")
REDUCE = ("xhi", "yhi", "core")
WHOLE = pl.BlockSpec(memory_space=pltpu.VMEM)
PARAMS = pltpu.CompilerParams(vmem_limit_bytes=24 << 20)


def far(value):
    return pltpu.with_memory_space_constraint(value, pltpu.HBM)


def near(value):
    return pltpu.with_memory_space_constraint(value, pltpu.VMEM)


def weigh_kernel(fields_ref, own_ref, out_ref):
    bands = own_ref.shape[-1]
    own_real = own_ref[0].astype(jnp.float32)
    own_imag = own_ref[1].astype(jnp.float32)
    for mode in range(out_ref.shape[-1] // bands):
        field_real = fields_ref[:, 2 * mode : 2 * mode + 1]
        field_imag = fields_ref[:, 2 * mode + 1 : 2 * mode + 2]
        cols = slice(mode * bands, (mode + 1) * bands)
        out_ref[0, :, cols] = (field_real * own_real - field_imag * own_imag).astype(jnp.bfloat16)
        out_ref[1, :, cols] = (field_real * own_imag + field_imag * own_real).astype(jnp.bfloat16)


def weigh(field, own, block=256):
    modes, _, rows = field.shape
    bands = own.shape[-1]
    columns = field.reshape(modes * 2, rows).astype(jnp.float32).T
    out = pl.pallas_call(
        weigh_kernel,
        grid=(rows // block,),
        in_specs=[
            pl.BlockSpec((block, modes * 2), lambda i: (i, 0)),
            pl.BlockSpec((2, block, bands), lambda i: (0, i, 0)),
        ],
        out_specs=pl.BlockSpec((2, block, modes * bands), lambda i: (0, i, 0)),
        out_shape=pltpu.HBM((2, rows, modes * bands), jnp.bfloat16),
        compiler_params=PARAMS,
        name="weigh",
    )(columns, own)
    return out.reshape(2 * rows, modes * bands)


def pick_kernel(partner_ref, spread_ref, out_hbm, out_ref, sems):
    points, _, num_q = out_ref.shape[:3]
    lanes = out_ref.shape[-1]
    quarter = lanes // 2
    step = points // sems.shape[0]
    low = lax.broadcasted_iota(jnp.int32, out_ref.shape[3:], 1) < quarter
    copies = []
    for at in range(points):
        for which in range(num_q):
            block = spread_ref[partner_ref[which, at]].astype(jnp.float32)
            left, right = block[:, :lanes], block[:, lanes:]
            even = jnp.where(low, left, pltpu.roll(right, quarter, 1))
            odd = jnp.where(low, pltpu.roll(left, quarter, 1), right)
            out_ref[at, 0, which] = even.astype(out_ref.dtype)
            out_ref[at, 1, which] = odd.astype(out_ref.dtype)
        if (at + 1) % step == 0:
            span = pl.ds(at + 1 - step, step)
            copies.append(pltpu.make_async_copy(out_ref.at[span], out_hbm.at[span], sems.at[at // step]))
            copies[-1].start()
    for copy in copies:
        copy.wait()


def pick(spread, partner):
    _, depth, bands = spread.shape
    num_q, points = partner.shape
    shape = (points, 2, num_q, depth, bands // 2)
    return pl.pallas_call(
        pick_kernel,
        grid_spec=pltpu.PrefetchScalarGridSpec(
            num_scalar_prefetch=1,
            grid=(),
            in_specs=[WHOLE],
            out_specs=pl.BlockSpec(memory_space=pltpu.HBM),
            scratch_shapes=[pltpu.VMEM(shape, spread.dtype), pltpu.SemaphoreType.DMA((8,))],
        ),
        out_shape=pltpu.HBM(shape, spread.dtype),
        compiler_params=PARAMS,
        name="pick",
    )(partner, near(spread))


def turn(fetched_ref, left_ref):
    bands = fetched_ref.shape[-1]
    turned = fetched_ref[...].reshape(-1, bands).T
    rows = turned.shape[1] // 2
    left_ref[:bands] = turned
    left_ref[bands:, :rows] = -turned[:, rows:]
    left_ref[bands:, rows:] = turned[:, :rows]


def couple_kernel(place_ref, fetched_hbm, own_ref, *refs):
    sides = fetched_hbm.shape[1]
    others_hbm, refs = refs[: sides - 1], refs[sides - 1 :]
    out_ref, fetched_ref, left_ref, sum_ref, others_ref, sems = refs
    pieces, rows, width = out_ref.shape
    block = width // 6
    incoming = [
        pltpu.make_async_copy(
            fetched_hbm.at[:, lax.bitwise_xor(place_ref[0], side)], fetched_ref.at[side], sems.at[0, side]
        )
        for side in range(sides)
    ]
    weights = [None] + [
        pltpu.make_async_copy(others_hbm[side - 1], others_ref.at[side - 1], sems.at[1, side])
        for side in range(1, sides)
    ]
    for copy in incoming[:2] + weights[1:2] + incoming[2:] + weights[2:3]:
        copy.start()
    for side in range(sides):
        incoming[side].wait()
        turn(fetched_ref.at[side], left_ref.at[side])
        if side:
            weights[side].wait()
            if side + 2 < sides:
                weights[side + 2].start()
        weighted_ref = others_ref.at[side - 1] if side else own_ref
        for start in range(0, width // 2, block):
            cols = slice(start, start + block)
            total = jnp.dot(left_ref[side], weighted_ref[:, cols], preferred_element_type=jnp.float32)
            if side:
                total += sum_ref[:, cols]
            if side < sides - 1:
                sum_ref[:, cols] = total
                continue
            total = total.astype(out_ref.dtype).reshape(2, pieces, rows, block)
            for part in range(2):
                at = 2 * start + part * block
                out_ref[:, :, at : at + block] = total[part]


def couple(place, fetched, own, others):
    points, sides, depth, bands = fetched.shape
    width = own.shape[-1]
    pieces = lax.axis_size(REDUCE)
    far_spec = pl.BlockSpec(memory_space=pltpu.HBM)
    return pl.pallas_call(
        couple_kernel,
        grid_spec=pltpu.PrefetchScalarGridSpec(
            num_scalar_prefetch=1,
            grid=(),
            in_specs=[far_spec, WHOLE] + [far_spec] * len(others),
            out_specs=WHOLE,
            scratch_shapes=[
                pltpu.VMEM((sides, points, depth, bands), fetched.dtype),
                pltpu.VMEM((sides, 2 * bands, points * depth), jnp.bfloat16),
                pltpu.VMEM((2 * bands, width), jnp.float32),
                pltpu.VMEM((len(others),) + own.shape, own.dtype),
                pltpu.SemaphoreType.DMA((2, sides)),
            ],
        ),
        out_shape=pltpu.VMEM((pieces, bands // pieces, 2 * width), jnp.bfloat16),
        compiler_params=PARAMS,
        name="couple",
    )(place.astype(jnp.int32).reshape(1), far(fetched), near(own), *[far(other) for other in others])


def final_kernel(parts_ref, out_ref):
    rows, num_q, modes, _, _, bands = out_ref.shape
    for which in range(num_q):
        for col in range(2 * modes):
            cols = slice(col * bands, (col + 1) * bands)
            total = parts_ref[which, :, cols].astype(jnp.float32)
            for source in range(which + num_q, parts_ref.shape[0], num_q):
                total = total + parts_ref[source, :, cols].astype(jnp.float32)
            for row in range(rows):
                out_ref[row, which, col // 2, col % 2] = total[row : row + 1]


def final(parts, num_q, modes):
    _, rows, width = parts.shape
    return pl.pallas_call(
        final_kernel,
        in_specs=[WHOLE],
        out_specs=WHOLE,
        out_shape=jax.ShapeDtypeStruct((rows, num_q, modes, 2, 1, width // (2 * modes)), jnp.float32),
        compiler_params=PARAMS,
        name="final",
    )(near(parts))


def exchange(value, axis):
    return lax.all_to_all(value, axis, split_axis=0, concat_axis=0, tiled=True)


def swap(value, axis):
    return lax.ppermute(value, axis, [(0, 1), (1, 0)])


def per_device(orbitals, fields, partner):
    num_q, modes = fields.shape[:2]
    own = orbitals[0]
    rows, bands = own.shape[1:]
    points = lax.axis_size(KA)
    depth = 2 * rows // points
    core = lax.axis_index("core")

    def of_q(values, which):
        return lax.dynamic_index_in_dim(values, which, 0, keepdims=False)

    spread = exchange(own.reshape(points, depth, bands), KA)
    across = swap(own, "xlo")
    across_fields = swap(fields, "xlo")
    beside = swap(own, "core")
    beside_field = swap(of_q(fields, 1 - core), "core")
    corner = swap(across, "core")
    corner_field = swap(of_q(across_fields, 1 - core), "core")
    own_weighted = weigh(of_q(fields, core), own)
    beside_weighted = weigh(beside_field, beside)
    across_weighted = weigh(of_q(across_fields, core), across)
    corner_weighted = weigh(corner_field, corner)
    picked = pick(spread, partner)
    fetched = exchange(picked.reshape(points * 2 * num_q, depth, bands // 2), KA + TEAM)
    product = couple(
        lax.axis_index(TEAM),
        fetched.reshape(points, 2 * num_q, depth, bands // 2),
        own_weighted,
        [beside_weighted, across_weighted, corner_weighted],
    )
    parts = exchange(product, REDUCE)
    return final(parts, num_q, modes)


def solution(mesh):
    fine = Mesh(mesh.devices.reshape(2, 8, 2, 2, 4, 2), KA + GRID)

    return jax.shard_map(
        per_device,
        mesh=fine,
        in_specs=(P(KA, None, GRID, None), P(None, None, None, GRID), P()),
        out_specs=P(GRID, None, None, None, KA, None),
        check_vma=False,
    )
```

```python
import jax
import jax.numpy as jnp
from jax import lax
from jax.experimental import pallas as pl
from jax.experimental.pallas import tpu as pltpu
from jax.sharding import Mesh, PartitionSpec as P


KA = ("ylo", "z")
GRID = ("xhi", "xlo", "yhi", "core")
TEAM = ("xlo", "core")
REDUCE = ("xhi", "yhi", "core")
WHOLE = pl.BlockSpec(memory_space=pltpu.VMEM)
PARAMS = pltpu.CompilerParams(vmem_limit_bytes=24 << 20)


def far(value):
    return pltpu.with_memory_space_constraint(value, pltpu.HBM)


def near(value):
    return pltpu.with_memory_space_constraint(value, pltpu.VMEM)


def weigh_kernel(fields_ref, own_ref, out_ref):
    bands = own_ref.shape[-1]
    own_real = own_ref[0].astype(jnp.float32)
    own_imag = own_ref[1].astype(jnp.float32)
    for mode in range(out_ref.shape[-1] // bands):
        field_real = fields_ref[:, 2 * mode : 2 * mode + 1]
        field_imag = fields_ref[:, 2 * mode + 1 : 2 * mode + 2]
        cols = slice(mode * bands, (mode + 1) * bands)
        out_ref[0, :, cols] = (field_real * own_real - field_imag * own_imag).astype(jnp.bfloat16)
        out_ref[1, :, cols] = (field_real * own_imag + field_imag * own_real).astype(jnp.bfloat16)


def weigh(field, own, block=256):
    modes, _, rows = field.shape
    bands = own.shape[-1]
    columns = field.reshape(modes * 2, rows).astype(jnp.float32).T
    out = pl.pallas_call(
        weigh_kernel,
        grid=(rows // block,),
        in_specs=[
            pl.BlockSpec((block, modes * 2), lambda i: (i, 0)),
            pl.BlockSpec((2, block, bands), lambda i: (0, i, 0)),
        ],
        out_specs=pl.BlockSpec((2, block, modes * bands), lambda i: (0, i, 0)),
        out_shape=pltpu.HBM((2, rows, modes * bands), jnp.bfloat16),
        compiler_params=PARAMS,
        name="weigh",
    )(columns, own)
    return out.reshape(2 * rows, modes * bands)


def pick_kernel(partner_ref, spread_ref, out_hbm, out_ref, sems):
    points, _, num_q = out_ref.shape[:3]
    lanes = out_ref.shape[-1]
    quarter = lanes // 2
    step = points // sems.shape[0]
    low = lax.broadcasted_iota(jnp.int32, out_ref.shape[3:], 1) < quarter
    copies = []
    for at in range(points):
        for which in range(num_q):
            block = spread_ref[partner_ref[which, at]].astype(jnp.float32)
            left, right = block[:, :lanes], block[:, lanes:]
            even = jnp.where(low, left, pltpu.roll(right, quarter, 1))
            odd = jnp.where(low, pltpu.roll(left, quarter, 1), right)
            out_ref[at, 0, which] = even.astype(out_ref.dtype)
            out_ref[at, 1, which] = odd.astype(out_ref.dtype)
        if (at + 1) % step == 0:
            span = pl.ds(at + 1 - step, step)
            copies.append(pltpu.make_async_copy(out_ref.at[span], out_hbm.at[span], sems.at[at // step]))
            copies[-1].start()
    for copy in copies:
        copy.wait()


def pick(spread, partner):
    _, depth, bands = spread.shape
    num_q, points = partner.shape
    shape = (points, 2, num_q, depth, bands // 2)
    return pl.pallas_call(
        pick_kernel,
        grid_spec=pltpu.PrefetchScalarGridSpec(
            num_scalar_prefetch=1,
            grid=(),
            in_specs=[WHOLE],
            out_specs=pl.BlockSpec(memory_space=pltpu.HBM),
            scratch_shapes=[pltpu.VMEM(shape, spread.dtype), pltpu.SemaphoreType.DMA((8,))],
        ),
        out_shape=pltpu.HBM(shape, spread.dtype),
        compiler_params=PARAMS,
        name="pick",
    )(partner, near(spread))


def turn(fetched_ref, left_ref):
    bands = fetched_ref.shape[-1]
    turned = fetched_ref[...].reshape(-1, bands).T
    rows = turned.shape[1] // 2
    left_ref[:bands] = turned
    left_ref[bands:, :rows] = -turned[:, rows:]
    left_ref[bands:, rows:] = turned[:, :rows]


def couple_kernel(place_ref, fetched_hbm, own_ref, *refs):
    sides = fetched_hbm.shape[1]
    others_hbm, refs = refs[: sides - 1], refs[sides - 1 :]
    out_ref, fetched_ref, left_ref, sum_ref, others_ref, sems = refs
    pieces, rows, width = out_ref.shape
    block = width // 6
    incoming = [
        pltpu.make_async_copy(
            fetched_hbm.at[:, lax.bitwise_xor(place_ref[0], side)], fetched_ref.at[side], sems.at[0, side]
        )
        for side in range(sides)
    ]
    weights = [None] + [
        pltpu.make_async_copy(others_hbm[side - 1], others_ref.at[side - 1], sems.at[1, side])
        for side in range(1, sides)
    ]
    for side in range(sides):
        incoming[side].start()
        if side:
            weights[side].start()
    for side in range(sides):
        incoming[side].wait()
        turn(fetched_ref.at[side], left_ref.at[side])
        if side:
            weights[side].wait()
        weighted_ref = others_ref.at[side - 1] if side else own_ref
        for start in range(0, width // 2, block):
            cols = slice(start, start + block)
            total = jnp.dot(left_ref[side], weighted_ref[:, cols], preferred_element_type=jnp.float32)
            if side:
                total += sum_ref[:, cols]
            if side < sides - 1:
                sum_ref[:, cols] = total
                continue
            total = total.astype(out_ref.dtype).reshape(2, pieces, rows, block)
            for part in range(2):
                at = 2 * start + part * block
                out_ref[:, :, at : at + block] = total[part]


def couple(place, fetched, own, others):
    points, sides, depth, bands = fetched.shape
    width = own.shape[-1]
    pieces = lax.axis_size(REDUCE)
    far_spec = pl.BlockSpec(memory_space=pltpu.HBM)
    return pl.pallas_call(
        couple_kernel,
        grid_spec=pltpu.PrefetchScalarGridSpec(
            num_scalar_prefetch=1,
            grid=(),
            in_specs=[far_spec, WHOLE] + [far_spec] * len(others),
            out_specs=WHOLE,
            scratch_shapes=[
                pltpu.VMEM((sides, points, depth, bands), fetched.dtype),
                pltpu.VMEM((sides, 2 * bands, points * depth), jnp.bfloat16),
                pltpu.VMEM((2 * bands, width), jnp.float32),
                pltpu.VMEM((len(others),) + own.shape, own.dtype),
                pltpu.SemaphoreType.DMA((2, sides)),
            ],
        ),
        out_shape=pltpu.VMEM((pieces, bands // pieces, 2 * width), jnp.bfloat16),
        compiler_params=PARAMS,
        name="couple",
    )(place.astype(jnp.int32).reshape(1), far(fetched), near(own), *[far(other) for other in others])


def final_kernel(parts_ref, out_ref):
    rows, num_q, modes, _, _, bands = out_ref.shape
    for which in range(num_q):
        for col in range(2 * modes):
            cols = slice(col * bands, (col + 1) * bands)
            total = parts_ref[which, :, cols].astype(jnp.float32)
            for source in range(which + num_q, parts_ref.shape[0], num_q):
                total = total + parts_ref[source, :, cols].astype(jnp.float32)
            for row in range(rows):
                out_ref[row, which, col // 2, col % 2] = total[row : row + 1]


def final(parts, num_q, modes):
    _, rows, width = parts.shape
    return pl.pallas_call(
        final_kernel,
        in_specs=[WHOLE],
        out_specs=WHOLE,
        out_shape=jax.ShapeDtypeStruct((rows, num_q, modes, 2, 1, width // (2 * modes)), jnp.float32),
        compiler_params=PARAMS,
        name="final",
    )(near(parts))


def exchange(value, axis):
    return lax.all_to_all(value, axis, split_axis=0, concat_axis=0, tiled=True)


def swap(value, axis):
    return lax.ppermute(value, axis, [(0, 1), (1, 0)])


def per_device(orbitals, fields, partner):
    num_q, modes = fields.shape[:2]
    own = orbitals[0]
    rows, bands = own.shape[1:]
    points = lax.axis_size(KA)
    depth = 2 * rows // points
    core = lax.axis_index("core")

    def of_q(values, which):
        return lax.dynamic_index_in_dim(values, which, 0, keepdims=False)

    spread = exchange(own.reshape(points, depth, bands), KA)
    across = swap(own, "xlo")
    across_fields = swap(fields, "xlo")
    beside = swap(own, "core")
    beside_field = swap(of_q(fields, 1 - core), "core")
    corner = swap(across, "core")
    corner_field = swap(of_q(across_fields, 1 - core), "core")
    own_weighted = weigh(of_q(fields, core), own)
    beside_weighted = weigh(beside_field, beside)
    across_weighted = weigh(of_q(across_fields, core), across)
    corner_weighted = weigh(corner_field, corner)
    picked = pick(spread, partner)
    fetched = exchange(picked.reshape(points * 2 * num_q, depth, bands // 2), KA + TEAM)
    product = couple(
        lax.axis_index(TEAM),
        fetched.reshape(points, 2 * num_q, depth, bands // 2),
        own_weighted,
        [beside_weighted, across_weighted, corner_weighted],
    )
    parts = exchange(product, REDUCE)
    return final(parts, num_q, modes)


def solution(mesh):
    fine = Mesh(mesh.devices.reshape(2, 8, 2, 2, 4, 2), KA + GRID)

    return jax.shard_map(
        per_device,
        mesh=fine,
        in_specs=(P(KA, None, GRID, None), P(None, None, None, GRID), P()),
        out_specs=P(GRID, None, None, None, KA, None),
        check_vma=False,
    )
```
